32 devices in a mesh: tm: 4 (over y, x), space: 8 (over z, core).
Axes of the slice: x: 2, y: 2, z: 4, core: 2. Of those that a mesh axis runs over, the one named last changes fastest.
Arguments:
- forcing: bfloat16 [16, 768, 6144], P('tm', 'space'), may hold values from -6 to 6
- conductivity: float32 [768, 6144], P('space'), may hold values from 0.5 to 2
- inverse_capacity: float32 [768, 6144], P('space'), may hold values from 0.03 to 0.12
- power_trace: float32 [16], P('tm'), may hold values from 0.2 to 2
- guess: float32 [4, 768, 6144], P('tm', 'space'), may hold values from -6 to 6
Outputs:
- power_gradient: float32 [768, 6144], P('space')
- block_starts: float32 [4, 768, 6144], P('tm', 'space')
The draws below stay inside these ranges and needn't reach their ends.
All inputs are finite; a program needn't handle non-finite values.
Results may differ from the reference program's by a relative error of at most 0.0003.
Values may be sent and summed in bfloat16 or wider, within the bound.
No kernel may reach another device: no remote copies, remote signals or barrier semaphores. Data moves between devices by JAX's collectives and lax.ppermute only.
A program may use at most 64 MiB of HBM per device.

```python
import math
import jax
import jax.numpy as jnp

COLS = 6144
BLOCK_STEPS = 4
ITERS = 2
NR = 768
TSTEPS = 16
N_TM = 4


def draw_forcing(key, part):
    values_out = jnp.clip(jax.random.normal(key, (TSTEPS, NR, COLS), jnp.float32), -6.0, 6.0)
    return values_out.astype(jnp.bfloat16)


def shard_levels(own_key, extent, shards, least, largest):
    factor_of, own = 1.0, jax.random.fold_in(own_key, 6)
    for dim, blocks in shards:
        steps = jnp.exp(jax.random.uniform(jax.random.fold_in(own, dim), (blocks,), jnp.float32, least / len(shards), largest / len(shards)))
        factor_of = factor_of * jnp.repeat(steps, extent[dim] // blocks).reshape([-1 if axis == dim else 1 for axis in range(len(extent))])
    return factor_of


def normal_values(stream_key, dims, spread, reach, split=(), dtype=jnp.bfloat16):
    gain = shard_levels(stream_key, dims, split, -0.22, 0.18) if split else 1.0
    array = jax.random.normal(stream_key, dims, jnp.float32) * spread * gain
    return jnp.minimum(jnp.maximum(array, -reach), reach).astype(dtype)


def setup_inputs(seed: int = 0) -> dict:
    keys = jax.random.split(jax.random.key(seed), 6)
    return {
        "forcing": draw_forcing(jax.random.fold_in(keys[5], 71), 0),
        "conductivity": jnp.clip(jnp.exp(math.log(2.0) - 1.3862944 * jax.random.uniform(keys[1], (NR, COLS), jnp.float32) ** shard_levels(keys[1], (NR, COLS), ((0, 8),), -0.2, 0.2)), 0.5, 2.0),
        "inverse_capacity": jnp.clip(jnp.exp(math.log(0.12) - 1.3862944 * jax.random.uniform(keys[2], (NR, COLS), jnp.float32) ** shard_levels(keys[2], (NR, COLS), ((0, 8),), -0.2, 0.2)), 0.03, 0.12),
        "power_trace": jnp.clip(jnp.exp(math.log(2.0) - 2.3025851 * jax.random.uniform(keys[3], (TSTEPS,), jnp.float32) ** shard_levels(keys[3], (TSTEPS,), ((0, 4),), -0.2, 0.2)), 0.2, 2.0),
        "guess": normal_values(keys[4], (N_TM, NR, COLS), 1.0, 6.0, ((0, 4), (1, 8)), jnp.float32),
    }


def pad_rows(values_in):
    config = [(0, 0)] * values_in.ndim
    config[values_in.ndim - 2] = (1, 1)
    return jnp.pad(values_in, config)


def pad_columns(values_in):
    config = [(0, 0)] * values_in.ndim
    config[values_in.ndim - 1] = (1, 1)
    return jnp.pad(values_in, config)


def apply_flow(middle, scaled, conduct):
    centre = scaled[..., 1:-1, :]
    inner_k = conduct[..., 1:-1, :]
    net_flow = 0.5 * (inner_k + conduct[..., :-2, :]) * (scaled[..., :-2, :] - centre)
    net_flow = net_flow + 0.5 * (inner_k + conduct[..., 2:, :]) * (scaled[..., 2:, :] - centre)
    side_scaled = pad_columns(centre)
    side_k = pad_columns(inner_k)
    net_flow = net_flow + 0.5 * (inner_k + side_k[..., :-2]) * (side_scaled[..., :-2] - centre)
    net_flow = net_flow + 0.5 * (inner_k + side_k[..., 2:]) * (side_scaled[..., 2:] - centre)
    return middle + net_flow


def reference(forcing, conductivity, inverse_capacity, power_trace, guess):
    source = forcing.reshape(N_TM, BLOCK_STEPS, NR, COLS)
    weights = power_trace.reshape(N_TM, BLOCK_STEPS)
    conduct_pad = pad_rows(conductivity)
    terminal = guess
    starts = guess
    gradient = jnp.zeros_like(guess)
    for sweep in range(ITERS):
        adjoint = terminal
        gradient = jnp.zeros_like(guess)
        for position in reversed(range(BLOCK_STEPS)):
            scaled = pad_rows(inverse_capacity * adjoint)
            adjoint = apply_flow(adjoint, scaled, conduct_pad) + source[:, position].astype(jnp.float32)
            gradient = gradient + weights[:, position][:, None, None] * adjoint
        starts = adjoint
        terminal = jnp.roll(starts, -1, axis=0)
    return jnp.sum(gradient, axis=0), starts
```

```python
import functools

import jax
import jax.numpy as jnp
from jax import lax
from jax.experimental import pallas as pl
from jax.experimental.pallas import tpu as pltpu
from jax.sharding import PartitionSpec as P

LANES = 128
HALO = 8
GUARD = 8
TAIL = 16
STATE_POWER = 9
STATE_SCALE = 128.0
SUM_POWER = 17
SUM_TOP = 160.0
VMEM = pltpu.VMEM
F32 = jnp.float32
BF16 = jnp.bfloat16


def power(z, degree):
    z2 = z * z
    z4 = z2 * z2
    z8 = z4 * z4
    return z8 * z if degree == 9 else (z8 * z8) * z


def root(y, degree):
    size = jnp.exp(jnp.log(jnp.abs(y)) * (1.0 / degree))
    return jnp.where(y < 0, -size, size)


def pack_rows(refs, out):
    forcing, rest = refs[0], refs[1:4]
    first = refs[4]
    for place, ref in enumerate(rest):
        value = ref[0] if len(ref.shape) == 3 else ref[...]
        high = value.astype(BF16).astype(F32)
        pair = jnp.concatenate([high, value - high], axis=0)
        out[pl.ds(place * 16, 16), :] = pair.astype(BF16)
    for step in range(0, forcing.shape[0], 2):
        pair = [forcing[step + one].astype(F32)[first : first + 8] for one in (0, 1)]
        out[pl.ds(48 + step * 8, 16), :] = jnp.concatenate(pair, axis=0).astype(BF16)


def pack_kernel(fl, gl, kl, cl, fh, gh, kh, ch, low, high):
    pack_rows((fl, gl, kl, cl, 0), low)
    pack_rows((fh, gh, kh, ch, 8), high)


def pack(forcing, guess, conductivity, capacity):
    steps, rows, cols = forcing.shape

    def specs(last):
        block = rows // 8 - 1 if last else 0
        return [
            pl.BlockSpec((steps, 16, cols), lambda i: (0, rows // 16 - 1 if last else 0, 0)),
            pl.BlockSpec((1, 8, cols), lambda i: (0, block, 0)),
            pl.BlockSpec((8, cols), lambda i: (block, 0)),
            pl.BlockSpec((8, cols), lambda i: (block, 0)),
        ]

    size = 48 + 8 * steps
    arrays = (forcing, guess, conductivity, capacity)
    return pl.pallas_call(
        pack_kernel,
        grid=(1,),
        in_specs=specs(False) + specs(True),
        out_specs=[pl.BlockSpec((size, cols), lambda i: (0, 0))] * 2,
        out_shape=[jax.ShapeDtypeStruct((size, cols), BF16)] * 2,
        name="pack",
    )(*arrays, *arrays)


def shifted(ref, j, rows, lane):
    centre = ref[j, rows]
    left = pltpu.roll(jnp.where(lane == LANES - 1, ref[j - 1, rows], centre), 1, 1)
    right = pltpu.roll(jnp.where(lane == 0, ref[j + 1, rows], centre), LANES - 1, 1)
    return centre, left, right


def block_kernel(
    first_tile, own_from, tiles, own_tiles, slots, rows,
    number, weight, forcing, conductivity, capacity, guess, top, bottom,
    state_out, forced_out, keep_out, send_out,
    cond, cap, one, two, three, four, total, c0, cu, cd, cl, cr, source, above, below, sem,
):
    steps = forcing.shape[0]
    lane = lax.broadcasted_iota(jnp.int32, (8, LANES), 1)
    base = GUARD + HALO
    end = base + rows
    bands = (end + HALO - GUARD) // 8
    copies = []

    def columns(j):
        return pl.ds(pl.multiple_of((first_tile + j) * LANES, LANES), LANES)

    def each(j, act):
        wide = columns(j)
        act(pltpu.make_async_copy(conductivity.at[:, wide], cond.at[j + 1, pl.ds(base, rows)], sem.at[0]))
        act(pltpu.make_async_copy(capacity.at[:, wide], cap.at[j + 1, pl.ds(base, rows)], sem.at[1]))
        act(pltpu.make_async_copy(guess.at[0, :, wide], one.at[j + 1, pl.ds(base, rows)], sem.at[2]))
        act(pltpu.make_async_copy(forcing.at[:, :, wide], source.at[j + 1], sem.at[3]))
        act(pltpu.make_async_copy(top.at[:, wide], above.at[j + 1], sem.at[4]))
        act(pltpu.make_async_copy(bottom.at[:, wide], below.at[j + 1], sem.at[5]))

    @pl.loop(0, tiles)
    def _(j):
        each(j, lambda copy: copy.start())

    blank = jnp.zeros((8, LANES), F32)
    for ref in (cond, one, two, three, four):
        for j in (0, tiles + 1):
            for i in range(bands + 2):
                ref[j, pl.ds(8 * i, 8)] = blank
        @pl.loop(0, tiles)
        def _(j):
            ref[j + 1, pl.ds(0, 8)] = blank
            ref[j + 1, pl.ds(end + HALO, 8)] = blank

    @pl.loop(0, tiles)
    def _(j):
        each(j, lambda copy: copy.wait())

    @pl.loop(1, tiles + 1)
    def _(j):
        for halo, row in ((above, GUARD), (below, end)):
            for ref, place in ((one, 0), (cond, 16), (cap, 32)):
                pair = halo[j, pl.ds(place, 16)].astype(F32)
                ref[j, pl.ds(row, 8)] = pair[:8] + pair[8:]

    @pl.loop(1, tiles + 1)
    def _(j):
        for i in range(1, bands + 1):
            at = pl.ds(8 * i, 8)
            k, left, right = shifted(cond, j, at, lane)
            own = cap[j, at]
            half = 0.5 * own
            to_left = half * (k + left)
            to_right = half * (k + right)
            to_up = half * (k + cond[j, pl.ds(8 * i - 1, 8)])
            to_down = half * (k + cond[j, pl.ds(8 * i + 1, 8)])
            cl[j, at] = to_left
            cr[j, at] = to_right
            cu[j, at] = to_up
            cd[j, at] = to_down
            c0[j, at] = 1.0 - ((to_left + to_right) + (to_up + to_down))
            one[j, at] = own * one[j, at]

    def moved(ref, j, i, near):
        at = pl.ds(8 * i, 8)
        centre, left, right = shifted(ref, j, at, lane)
        up = ref[j, pl.ds(8 * i - 1, 8)]
        down = ref[j, pl.ds(8 * i + 1, 8)]
        k0, ku, kd, kl, kr = near
        return (k0 * centre + ku * up) + (kd * down + (kl * left + kr * right))

    def near(j, i):
        at = pl.ds(8 * i, 8)
        return tuple(ref[j, at] for ref in (c0, cu, cd, cl, cr))

    def forced(j, i, step):
        at = pl.ds(8 * i, 8)
        if i == 1 or i == bands:
            halo = above if i == 1 else below
            pair = halo[j, pl.ds(48 + 16 * (step // 2), 16)].astype(F32)
            value = pair[8 * (step % 2) : 8 * (step % 2) + 8]
        else:
            row = 8 * (i - 2)
            pair = source[j, step, pl.ds(row // 16 * 16, 16)].astype(F32)
            value = pair[row % 16 : row % 16 + 8]
        return cap[j, at] * value

    here, there = one, two
    from_zero, next_zero = three, four
    for step in reversed(range(steps)):
        opening = step == steps - 1
        share = weight[0, step]

        @pl.loop(1, tiles + 1)
        def _(j):
            for i in range(1, bands + 1):
                at = pl.ds(8 * i, 8)
                push = forced(j, i, step)
                beside = near(j, i)
                there[j, at] = moved(here, j, i, beside) + push
                if opening:
                    zero_state = push
                    total[j, at] = share * push
                else:
                    zero_state = moved(from_zero, j, i, beside) + push
                    total[j, at] = total[j, at] + share * zero_state
                next_zero[j, at] = zero_state

        here, there = there, here
        from_zero, next_zero = next_zero, from_zero

    for step in reversed(range(steps)):
        share = weight[1, step]

        @pl.loop(1, tiles + 1)
        def _(j):
            for i in range(1, bands + 1):
                at = pl.ds(8 * i, 8)
                value = moved(here, j, i, near(j, i))
                there[j, at] = value
                total[j, at] = total[j, at] + share * value

        here, there = there, here

    def finish(n, high):
        j = n + own_from + 1
        for i in range(rows // 16):
            at = pl.ds(base + 16 * i, 16)
            out = pl.ds(pl.multiple_of(n * rows + 16 * i, 16), 16)
            inverse = 1.0 / cap[j, at]
            state_out[out] = power(here[j, at] * inverse * STATE_SCALE, STATE_POWER).astype(BF16)
            forced_out[out] = from_zero[j, at] * inverse
            value = total[j, at] * inverse
            total[j, at] = value
            size = jnp.abs(value)
            high = jnp.maximum(high, jnp.maximum(size[:8], size[8:]))
        return high

    high = lax.fori_loop(0, own_tiles, finish, jnp.zeros((8, LANES), F32))
    level = jnp.full((TAIL, LANES), jnp.maximum(jnp.max(high), 1e-30) * 1.01, F32).astype(BF16)
    per = own_tiles // slots
    send_out[pl.ds(slots // 2 * per * rows, TAIL)] = level
    scale = SUM_TOP / level.astype(F32)
    for slot in range(slots):
        source_slot = jnp.bitwise_xor(number[0], slot)

        @pl.loop(0, per)
        def _(n):
            j = source_slot * per + n + own_from + 1
            for i in range(rows // 16):
                value = total[j, pl.ds(base + 16 * i, 16)]
                place = slot % (slots // 2) * per + n
                out = pl.ds(pl.multiple_of(place * rows + 16 * i, 16), 16)
                if slot < slots // 2:
                    keep_out[out] = value
                else:
                    send_out[out] = power(value * scale, SUM_POWER).astype(BF16)


def block(part, parts, slots, number, weight, forcing, conductivity, capacity, guess, top, bottom):
    steps, rows, cols = forcing.shape
    all_tiles = cols // LANES
    own = all_tiles // parts
    low = max(part * own - 1, 0)
    high = min((part + 1) * own + 1, all_tiles)
    tiles = high - low
    depth = rows + 2 * (HALO + GUARD)
    size = own * rows
    whole = pltpu.VMEM((tiles + 2, depth, LANES), F32)
    halo = pltpu.VMEM((tiles + 2, top.shape[0], LANES), BF16)
    return pl.pallas_call(
        functools.partial(block_kernel, low, part * own - low, tiles, own, slots, rows),
        in_specs=[pl.BlockSpec(memory_space=pltpu.SMEM)] * 2 + [pl.BlockSpec(memory_space=pl.ANY)] * 6,
        out_specs=[pl.BlockSpec(memory_space=VMEM)] * 4,
        out_shape=[
            jax.ShapeDtypeStruct((size, LANES), BF16),
            jax.ShapeDtypeStruct((size, LANES), F32),
            jax.ShapeDtypeStruct((size // 2, LANES), F32),
            jax.ShapeDtypeStruct((size // 2 + TAIL, LANES), BF16),
        ],
        scratch_shapes=[whole] * 12
        + [pltpu.VMEM((tiles + 2, steps, rows, LANES), BF16), halo, halo, pltpu.SemaphoreType.DMA((6,))],
        compiler_params=pltpu.CompilerParams(vmem_limit_bytes=60 << 20),
        cost_estimate=pl.CostEstimate(flops=size * LANES * 200, bytes_accessed=size * LANES * 30, transcendentals=0),
        name="block",
    )(number, weight, forcing, conductivity, capacity, guess, top, bottom)


def add_kernel(keep, got, *refs):
    rest, send, hold = refs[:-2], refs[-2], refs[-1]
    size = keep.shape[0]
    kept = size // 2 if rest else 0
    sent = size - kept
    scale = got[pl.ds(size, TAIL)].astype(F32) * (1.0 / SUM_TOP)

    def value_at(row):
        at = pl.ds(pl.multiple_of(row, 16), 16)
        return keep[at] + root(got[at].astype(F32), SUM_POWER) * scale

    def measure(i, high):
        value = value_at(kept + 16 * i)
        hold[pl.ds(pl.multiple_of(16 * i, 16), 16)] = value
        return jnp.maximum(high, jnp.abs(value))

    high = lax.fori_loop(0, sent // 16, measure, jnp.zeros((16, LANES), F32), unroll=6)
    level = jnp.full((TAIL, LANES), jnp.maximum(jnp.max(high), 1e-30) * 1.01, F32).astype(BF16)
    send[pl.ds(sent, TAIL)] = level
    up = SUM_TOP / level.astype(F32)

    @pl.loop(0, sent // 16, unroll=6)
    def _(i):
        at = pl.ds(pl.multiple_of(16 * i, 16), 16)
        send[at] = power(hold[at] * up, SUM_POWER).astype(BF16)

    if rest:
        @pl.loop(0, kept // 16, unroll=6)
        def _(i):
            rest[0][pl.ds(pl.multiple_of(16 * i, 16), 16)] = value_at(16 * i)


def add(keep, got, last):
    size = keep.shape[0]
    sent = size if last else size // 2
    shapes = [] if last else [jax.ShapeDtypeStruct((size - sent, LANES), F32)]
    shapes = shapes + [jax.ShapeDtypeStruct((sent + TAIL, LANES), BF16)]
    return pl.pallas_call(
        add_kernel,
        in_specs=[pl.BlockSpec(memory_space=VMEM)] * 2,
        out_specs=[pl.BlockSpec(memory_space=VMEM)] * len(shapes),
        out_shape=shapes,
        scratch_shapes=[pltpu.VMEM((sent, LANES), F32)],
        cost_estimate=pl.CostEstimate(flops=size * LANES * 20, bytes_accessed=size * LANES * 8, transcendentals=0),
        name="add",
    )(keep, got)


def gradient_kernel(parts, slots, rows, number, *refs):
    out = refs[-1]
    for part in range(parts):
        for slot in range(slots):
            ref = refs[part * slots + slot]
            tiles = (ref.shape[0] - TAIL) // rows
            place = jnp.bitwise_xor(number[part], slot)
            scale = ref[pl.ds(tiles * rows, TAIL)].astype(F32) * (1.0 / SUM_TOP)

            @pl.loop(0, tiles)
            def _(n):
                tile = part * slots * tiles + place * tiles + n
                wide = pl.ds(pl.multiple_of(tile * LANES, LANES), LANES)
                for i in range(rows // 16):
                    coded = ref[pl.ds(pl.multiple_of(n * rows + 16 * i, 16), 16)]
                    out[pl.ds(16 * i, 16), wide] = root(coded.astype(F32), SUM_POWER) * scale


def gradient_of(number, payloads, rows, cols):
    parts, slots = len(payloads), len(payloads[0])
    flat = [one for some in payloads for one in some]
    return pl.pallas_call(
        functools.partial(gradient_kernel, parts, slots, rows),
        in_specs=[pl.BlockSpec(memory_space=pltpu.SMEM)] + [pl.BlockSpec(memory_space=VMEM)] * len(flat),
        out_specs=pl.BlockSpec(memory_space=VMEM),
        out_shape=jax.ShapeDtypeStruct((rows, cols), F32),
        cost_estimate=pl.CostEstimate(flops=rows * cols * 20, bytes_accessed=rows * cols * 6, transcendentals=0),
        name="gradient",
    )(number, *flat)


def starts_kernel(parts, rows, *refs):
    out = refs[-1]
    for part in range(parts):
        got, forced = refs[2 * part], refs[2 * part + 1]
        tiles = got.shape[0] // rows

        @pl.loop(0, tiles)
        def _(n):
            wide = pl.ds(pl.multiple_of((part * tiles + n) * LANES, LANES), LANES)
            for i in range(rows // 16):
                at = pl.ds(pl.multiple_of(n * rows + 16 * i, 16), 16)
                state = root(got[at].astype(F32), STATE_POWER) * (1.0 / STATE_SCALE)
                out[pl.ds(16 * i, 16), wide] = state + forced[at]


def starts_of(pairs, rows, cols):
    flat = [one for pair in pairs for one in pair]
    return pl.pallas_call(
        functools.partial(starts_kernel, len(pairs), rows),
        in_specs=[pl.BlockSpec(memory_space=VMEM)] * len(flat),
        out_specs=pl.BlockSpec(memory_space=VMEM),
        out_shape=jax.ShapeDtypeStruct((rows, cols), F32),
        cost_estimate=pl.CostEstimate(flops=rows * cols * 20, bytes_accessed=rows * cols * 10, transcendentals=0),
        name="starts",
    )(*flat)


def local(forcing, conductivity, inverse_capacity, power_trace, guess):
    steps, rows, cols = forcing.shape
    blocks = lax.axis_size("tm")
    strips = lax.axis_size("space")
    bits = blocks.bit_length() - 1
    ring = [(b, (b + 1) % blocks) for b in range(blocks)]
    back = [(target, source) for source, target in ring]
    line = [(i, i + 1) for i in range(strips - 1)]
    upward = [(target, source) for source, target in line]

    before = lax.ppermute(power_trace, "tm", ring)
    weight = jnp.stack([power_trace, before])
    low, high = pack(forcing, guess, conductivity, inverse_capacity)
    top = lax.ppermute(high, "space", line)
    bottom = lax.ppermute(low, "space", upward)

    mine = lax.axis_index("tm")
    orders = [list(reversed(range(bits))), list(range(bits))]
    numbers = []
    for order in orders:
        number = jnp.zeros((), jnp.int32)
        for bit in order:
            number = number * 2 + (mine >> bit) % 2
        numbers.append(number)
    numbers = jnp.stack(numbers)

    def swap(value, bit):
        return lax.ppermute(value, "tm", [(b, b ^ (1 << bit)) for b in range(blocks)])

    results = []
    for part, order in enumerate(orders):
        state, forced, keep, send = block(
            part, len(orders), blocks, numbers[part : part + 1], weight,
            forcing, conductivity, inverse_capacity, guess, top, bottom,
        )
        results.append((state, forced, keep, send))
    pairs, payloads = [], []
    for part, order in enumerate(orders):
        state, forced, keep, send = results[part]
        for place, bit in enumerate(order):
            got = swap(send, bit)
            if place + 1 < bits:
                keep, send = add(keep, got, False)
            else:
                (send,) = add(keep, got, True)
        held = [send]
        for bit in reversed(order):
            held = held + [swap(one, bit) for one in held]
        payloads.append(held)
        pairs.append((lax.ppermute(state, "tm", back), forced))
    return (gradient_of(numbers, payloads, rows, cols), starts_of(pairs, rows, cols)[None])


def solution(mesh):
    in_specs = (
        P("tm", "space", None),
        P("space", None),
        P("space", None),
        P("tm"),
        P("tm", "space", None),
    )
    out_specs = (P("space", None), P("tm", "space", None))
    return jax.shard_map(local, mesh=mesh, in_specs=in_specs, out_specs=out_specs, check_vma=False)
```

```python
import functools

import jax
import jax.numpy as jnp
from jax import lax
from jax.experimental import pallas as pl
from jax.experimental.pallas import tpu as pltpu
from jax.sharding import PartitionSpec as P

LANES = 128
HALO = 8
GUARD = 8
TAIL = 16
STATE_POWER = 9
STATE_SCALE = 128.0
SUM_POWER = 17
SUM_TOP = 160.0
VMEM = pltpu.VMEM
F32 = jnp.float32
BF16 = jnp.bfloat16


def power(z, degree):
    z2 = z * z
    z4 = z2 * z2
    z8 = z4 * z4
    return z8 * z if degree == 9 else (z8 * z8) * z


def root(y, degree):
    size = jnp.exp(jnp.log(jnp.abs(y)) * (1.0 / degree))
    return jnp.where(y < 0, -size, size)


def pack_rows(refs, out):
    forcing, rest = refs[0], refs[1:4]
    first = refs[4]
    for place, ref in enumerate(rest):
        value = ref[0] if len(ref.shape) == 3 else ref[...]
        high = value.astype(BF16).astype(F32)
        pair = jnp.concatenate([high, value - high], axis=0)
        out[pl.ds(place * 16, 16), :] = pair.astype(BF16)
    for step in range(0, forcing.shape[0], 2):
        pair = [forcing[step + one].astype(F32)[first : first + 8] for one in (0, 1)]
        out[pl.ds(48 + step * 8, 16), :] = jnp.concatenate(pair, axis=0).astype(BF16)


def pack_kernel(fl, gl, kl, cl, fh, gh, kh, ch, low, high):
    pack_rows((fl, gl, kl, cl, 0), low)
    pack_rows((fh, gh, kh, ch, 8), high)


def pack(forcing, guess, conductivity, capacity):
    steps, rows, cols = forcing.shape

    def specs(last):
        block = rows // 8 - 1 if last else 0
        return [
            pl.BlockSpec((steps, 16, cols), lambda i: (0, rows // 16 - 1 if last else 0, 0)),
            pl.BlockSpec((1, 8, cols), lambda i: (0, block, 0)),
            pl.BlockSpec((8, cols), lambda i: (block, 0)),
            pl.BlockSpec((8, cols), lambda i: (block, 0)),
        ]

    size = 48 + 8 * steps
    arrays = (forcing, guess, conductivity, capacity)
    return pl.pallas_call(
        pack_kernel,
        grid=(1,),
        in_specs=specs(False) + specs(True),
        out_specs=[pl.BlockSpec((size, cols), lambda i: (0, 0))] * 2,
        out_shape=[jax.ShapeDtypeStruct((size, cols), BF16)] * 2,
        name="pack",
    )(*arrays, *arrays)


def neighbours(values, lane):
    triples = []
    for before, centre, after in zip(values, values[1:], values[2:]):
        left = pltpu.roll(jnp.where(lane == LANES - 1, before, centre), 1, 1)
        right = pltpu.roll(jnp.where(lane == 0, after, centre), LANES - 1, 1)
        triples.append((centre, left, right))
    return triples


def block_kernel(
    first_tile, own_from, tiles, own_tiles, slots, rows, group,
    number, weight, forcing, conductivity, capacity, guess, top, bottom,
    state_out, forced_out, keep_out, send_out,
    cond, cap, one, two, zeros, nexts, total, c0, cu, cd, cl, cr, source, sem,
):
    steps = forcing.shape[0]
    groups = tiles // group
    lane = lax.broadcasted_iota(jnp.int32, (8, LANES), 1)
    base = GUARD + HALO
    end = base + rows
    bands = (end + HALO - GUARD) // 8
    every = range(1, bands + 1)
    inner = range(2, bands)

    def columns(j):
        return pl.ds(pl.multiple_of((first_tile + j) * LANES, LANES), LANES)

    def each(j, g, act):
        wide = columns(j)
        act(pltpu.make_async_copy(conductivity.at[:, wide], cond.at[j + 1, pl.ds(base, rows)], sem.at[0, g]))
        act(pltpu.make_async_copy(capacity.at[:, wide], cap.at[j + 1, pl.ds(base, rows)], sem.at[1, g]))
        act(pltpu.make_async_copy(guess.at[0, :, wide], one.at[j + 1, pl.ds(base, rows)], sem.at[2, g]))
        act(pltpu.make_async_copy(forcing.at[:, :, wide], source.at[j + 1], sem.at[3, g]))

    def wait(g):
        for u in range(group):
            each(g * group + u, g, lambda copy: copy.wait())

    @pl.loop(0, tiles)
    def _(j):
        each(j, j // group, lambda copy: copy.start())

    blank = jnp.zeros((8, LANES), F32)
    level_refs = [zeros.at[k] for k in range(steps)] + [nexts.at[k] for k in range(steps)]
    for ref in [cond, one, two] + level_refs:
        for j in (0, tiles + 1):
            for i in range(bands + 2):
                ref[j, pl.ds(8 * i, 8)] = blank

    @pl.loop(1, tiles + 1)
    def _(j):
        for ref in [cond, one, two] + level_refs:
            ref[j, pl.ds(0, 8)] = blank
            ref[j, pl.ds(end + HALO, 8)] = blank
        wide = pl.ds(pl.multiple_of((first_tile + j - 1) * LANES, LANES), LANES)
        for halo, row in ((top, GUARD), (bottom, end)):
            for ref, place in ((one, 0), (cond, 16), (cap, 32)):
                pair = halo[pl.ds(place, 16), wide].astype(F32)
                ref[j, pl.ds(row, 8)] = pair[:8] + pair[8:]

    wait(0)

    @pl.loop(0, groups)
    def _(g):
        @pl.when(g + 1 < groups)
        def _():
            wait(g + 1)

        for i in every:
            at = pl.ds(8 * i, 8)
            values = [cond[g * group + u, at] for u in range(group + 2)]
            for u, (k, left, right) in enumerate(neighbours(values, lane)):
                j = g * group + u + 1
                own = cap[j, at]
                half = 0.5 * own
                to_left = half * (k + left)
                to_right = half * (k + right)
                to_up = half * (k + cond[j, pl.ds(8 * i - 1, 8)])
                to_down = half * (k + cond[j, pl.ds(8 * i + 1, 8)])
                cl[j, at] = to_left
                cr[j, at] = to_right
                cu[j, at] = to_up
                cd[j, at] = to_down
                c0[j, at] = 1.0 - ((to_left + to_right) + (to_up + to_down))
                one[j, at] = own * one[j, at]

    def pushes(j, pair, step):
        if len(pair) == 1:
            halo = top if pair[0] == 1 else bottom
            wide = pl.ds(pl.multiple_of((first_tile + j - 1) * LANES, LANES), LANES)
            both = halo[pl.ds(48 + 16 * (step // 2), 16), wide].astype(F32)
            return [cap[j, pl.ds(8 * pair[0], 8)] * both[8 * (step % 2) : 8 * (step % 2) + 8]]
        row = 8 * (pair[0] - 2)
        both = source[j, step, pl.ds(row, 16)].astype(F32)
        return [cap[j, pl.ds(8 * i, 8)] * both[8 * k : 8 * k + 8] for k, i in enumerate(pair)]

    def apply(states, outs, step, bands_of):
        pairs = [(1,)] + [(i, i + 1) for i in range(2, bands, 2)] + [(bands,)]

        @pl.loop(0, groups)
        def _(g):
            first = g * group
            for pair in pairs:
                push = [pushes(first + u + 1, pair, step) for u in range(group)] if step is not None else None
                for k, i in enumerate(pair):
                    at = pl.ds(8 * i, 8)
                    active = [n for n in range(len(outs)) if i in bands_of[n]]
                    if not active:
                        continue
                    around = {
                        n: neighbours([states[n][first + u, at] for u in range(group + 2)], lane)
                        for n in active if states[n] is not None
                    }
                    for u in range(group):
                        j = first + u + 1
                        near = tuple(ref[j, at] for ref in (c0, cu, cd, cl, cr)) if around else None
                        for n in active:
                            if states[n] is None:
                                outs[n][j, at] = push[u][k]
                                continue
                            centre, left, right = around[n][u]
                            up = states[n][j, pl.ds(8 * i - 1, 8)]
                            down = states[n][j, pl.ds(8 * i + 1, 8)]
                            k0, ku, kd, kl, kr = near
                            value = (k0 * centre + ku * up) + (kd * down + (kl * left + kr * right))
                            outs[n][j, at] = value + push[u][k] if step is not None else value

    here, there = one, two
    before = None
    for count, step in enumerate(reversed(range(steps))):
        closing = step == 0
        apply([here, before], [there, zeros.at[count]], step, [every, inner if closing else every])
        here, there = there, here
        before = zeros.at[count]
    for count in range(steps):
        apply([here], [nexts.at[count]], None, [inner if count == steps - 1 else every])
        here = nexts.at[count]

    def finish(n, high):
        j = n + own_from + 1
        for i in range(rows // 16):
            at = pl.ds(base + 16 * i, 16)
            out = pl.ds(pl.multiple_of(n * rows + 16 * i, 16), 16)
            inverse = 1.0 / cap[j, at]
            last = nexts[steps - 1, j, at]
            state_out[out] = power(last * inverse * STATE_SCALE, STATE_POWER).astype(BF16)
            forced_last = zeros[steps - 1, j, at]
            forced_out[out] = forced_last * inverse
            value = weight[0, 0] * forced_last + weight[1, 0] * last
            for count in range(steps - 1):
                step = steps - 1 - count
                value = value + (weight[0, step] * zeros[count, j, at] + weight[1, step] * nexts[count, j, at])
            value = value * inverse
            total[j, at] = value
            size = jnp.abs(value)
            high = jnp.maximum(high, jnp.maximum(size[:8], size[8:]))
        return high

    high = lax.fori_loop(0, own_tiles, finish, jnp.zeros((8, LANES), F32), unroll=2)
    level = jnp.full((TAIL, LANES), jnp.maximum(jnp.max(high), 1e-30) * 1.01, F32).astype(BF16)
    per = own_tiles // slots
    send_out[pl.ds(slots // 2 * per * rows, TAIL)] = level
    scale = SUM_TOP / level.astype(F32)
    for slot in range(slots):
        source_slot = jnp.bitwise_xor(number[0], slot)

        @pl.loop(0, per, unroll=3)
        def _(n):
            j = source_slot * per + n + own_from + 1
            for i in range(rows // 16):
                value = total[j, pl.ds(base + 16 * i, 16)]
                place = slot % (slots // 2) * per + n
                out = pl.ds(pl.multiple_of(place * rows + 16 * i, 16), 16)
                if slot < slots // 2:
                    keep_out[out] = value
                else:
                    send_out[out] = power(value * scale, SUM_POWER).astype(BF16)


def group_size(tiles):
    return max(size for size in range(1, 7) if tiles % size == 0)


def block(part, parts, slots, number, weight, forcing, conductivity, capacity, guess, top, bottom):
    steps, rows, cols = forcing.shape
    all_tiles = cols // LANES
    own = all_tiles // parts
    low = max(part * own - 1, 0)
    high = min((part + 1) * own + 1, all_tiles)
    tiles = high - low
    group = group_size(tiles)
    depth = rows + 2 * (HALO + GUARD)
    size = own * rows
    whole = pltpu.VMEM((tiles + 2, depth, LANES), F32)
    levels = pltpu.VMEM((steps, tiles + 2, depth, LANES), F32)
    return pl.pallas_call(
        functools.partial(block_kernel, low, part * own - low, tiles, own, slots, rows, group),
        in_specs=[pl.BlockSpec(memory_space=pltpu.SMEM)] * 2
        + [pl.BlockSpec(memory_space=pl.ANY)] * 4
        + [pl.BlockSpec(memory_space=VMEM)] * 2,
        out_specs=[pl.BlockSpec(memory_space=VMEM)] * 4,
        out_shape=[
            jax.ShapeDtypeStruct((size, LANES), BF16),
            jax.ShapeDtypeStruct((size, LANES), F32),
            jax.ShapeDtypeStruct((size // 2, LANES), F32),
            jax.ShapeDtypeStruct((size // 2 + TAIL, LANES), BF16),
        ],
        scratch_shapes=[whole] * 4 + [levels] * 2 + [whole] * 6
        + [pltpu.VMEM((tiles + 2, steps, rows, LANES), BF16), pltpu.SemaphoreType.DMA((4, tiles // group))],
        compiler_params=pltpu.CompilerParams(vmem_limit_bytes=60 << 20),
        cost_estimate=pl.CostEstimate(flops=size * LANES * 200, bytes_accessed=size * LANES * 30, transcendentals=0),
        name="block",
    )(number, weight, forcing, conductivity, capacity, guess, top, bottom)


def add_kernel(keep, got, *refs):
    rest, send, hold = refs[:-2], refs[-2], refs[-1]
    size = keep.shape[0]
    kept = size // 2 if rest else 0
    sent = size - kept
    scale = got[pl.ds(size, TAIL)].astype(F32) * (1.0 / SUM_TOP)

    def value_at(row):
        at = pl.ds(pl.multiple_of(row, 16), 16)
        return keep[at] + root(got[at].astype(F32), SUM_POWER) * scale

    def measure(i, high):
        value = value_at(kept + 16 * i)
        hold[pl.ds(pl.multiple_of(16 * i, 16), 16)] = value
        return jnp.maximum(high, jnp.abs(value))

    high = lax.fori_loop(0, sent // 16, measure, jnp.zeros((16, LANES), F32), unroll=6)
    level = jnp.full((TAIL, LANES), jnp.maximum(jnp.max(high), 1e-30) * 1.01, F32).astype(BF16)
    send[pl.ds(sent, TAIL)] = level
    up = SUM_TOP / level.astype(F32)

    @pl.loop(0, sent // 16, unroll=6)
    def _(i):
        at = pl.ds(pl.multiple_of(16 * i, 16), 16)
        send[at] = power(hold[at] * up, SUM_POWER).astype(BF16)

    if rest:
        @pl.loop(0, kept // 16, unroll=6)
        def _(i):
            rest[0][pl.ds(pl.multiple_of(16 * i, 16), 16)] = value_at(16 * i)


def add(keep, got, last):
    size = keep.shape[0]
    sent = size if last else size // 2
    shapes = [] if last else [jax.ShapeDtypeStruct((size - sent, LANES), F32)]
    shapes = shapes + [jax.ShapeDtypeStruct((sent + TAIL, LANES), BF16)]
    return pl.pallas_call(
        add_kernel,
        in_specs=[pl.BlockSpec(memory_space=VMEM)] * 2,
        out_specs=[pl.BlockSpec(memory_space=VMEM)] * len(shapes),
        out_shape=shapes,
        scratch_shapes=[pltpu.VMEM((sent, LANES), F32)],
        cost_estimate=pl.CostEstimate(flops=size * LANES * 20, bytes_accessed=size * LANES * 8, transcendentals=0),
        name="add",
    )(keep, got)


def gradient_kernel(parts, slots, rows, number, *refs):
    out = refs[-1]
    for part in range(parts):
        for slot in range(slots):
            ref = refs[part * slots + slot]
            tiles = (ref.shape[0] - TAIL) // rows
            place = jnp.bitwise_xor(number[part], slot)
            scale = ref[pl.ds(tiles * rows, TAIL)].astype(F32) * (1.0 / SUM_TOP)

            @pl.loop(0, tiles)
            def _(n):
                tile = part * slots * tiles + place * tiles + n
                wide = pl.ds(pl.multiple_of(tile * LANES, LANES), LANES)
                for i in range(rows // 16):
                    coded = ref[pl.ds(pl.multiple_of(n * rows + 16 * i, 16), 16)]
                    out[pl.ds(16 * i, 16), wide] = root(coded.astype(F32), SUM_POWER) * scale


def gradient_of(number, payloads, rows, cols):
    parts, slots = len(payloads), len(payloads[0])
    flat = [one for some in payloads for one in some]
    return pl.pallas_call(
        functools.partial(gradient_kernel, parts, slots, rows),
        in_specs=[pl.BlockSpec(memory_space=pltpu.SMEM)] + [pl.BlockSpec(memory_space=VMEM)] * len(flat),
        out_specs=pl.BlockSpec(memory_space=VMEM),
        out_shape=jax.ShapeDtypeStruct((rows, cols), F32),
        cost_estimate=pl.CostEstimate(flops=rows * cols * 20, bytes_accessed=rows * cols * 6, transcendentals=0),
        name="gradient",
    )(number, *flat)


def starts_kernel(parts, rows, *refs):
    out = refs[-1]
    for part in range(parts):
        got, forced = refs[2 * part], refs[2 * part + 1]
        tiles = got.shape[0] // rows

        @pl.loop(0, tiles)
        def _(n):
            wide = pl.ds(pl.multiple_of((part * tiles + n) * LANES, LANES), LANES)
            for i in range(rows // 16):
                at = pl.ds(pl.multiple_of(n * rows + 16 * i, 16), 16)
                state = root(got[at].astype(F32), STATE_POWER) * (1.0 / STATE_SCALE)
                out[pl.ds(16 * i, 16), wide] = state + forced[at]


def starts_of(pairs, rows, cols):
    flat = [one for pair in pairs for one in pair]
    return pl.pallas_call(
        functools.partial(starts_kernel, len(pairs), rows),
        in_specs=[pl.BlockSpec(memory_space=VMEM)] * len(flat),
        out_specs=pl.BlockSpec(memory_space=VMEM),
        out_shape=jax.ShapeDtypeStruct((rows, cols), F32),
        cost_estimate=pl.CostEstimate(flops=rows * cols * 20, bytes_accessed=rows * cols * 10, transcendentals=0),
        name="starts",
    )(*flat)


def local(forcing, conductivity, inverse_capacity, power_trace, guess):
    steps, rows, cols = forcing.shape
    blocks = lax.axis_size("tm")
    strips = lax.axis_size("space")
    bits = blocks.bit_length() - 1
    ring = [(b, (b + 1) % blocks) for b in range(blocks)]
    back = [(target, source) for source, target in ring]
    line = [(i, i + 1) for i in range(strips - 1)]
    upward = [(target, source) for source, target in line]

    before = lax.ppermute(power_trace, "tm", ring)
    weight = jnp.stack([power_trace, before])
    low, high = pack(forcing, guess, conductivity, inverse_capacity)
    top = lax.ppermute(high, "space", line)
    bottom = lax.ppermute(low, "space", upward)

    mine = lax.axis_index("tm")
    orders = [list(reversed(range(bits))), list(range(bits))]
    numbers = []
    for order in orders:
        number = jnp.zeros((), jnp.int32)
        for bit in order:
            number = number * 2 + (mine >> bit) % 2
        numbers.append(number)
    numbers = jnp.stack(numbers)

    def swap(value, bit):
        return lax.ppermute(value, "tm", [(b, b ^ (1 << bit)) for b in range(blocks)])

    results = []
    for part, order in enumerate(orders):
        state, forced, keep, send = block(
            part, len(orders), blocks, numbers[part : part + 1], weight,
            forcing, conductivity, inverse_capacity, guess, top, bottom,
        )
        results.append((state, forced, keep, send))
    pairs, payloads = [], []
    for part, order in enumerate(orders):
        state, forced, keep, send = results[part]
        for place, bit in enumerate(order):
            got = swap(send, bit)
            if place + 1 < bits:
                keep, send = add(keep, got, False)
            else:
                (send,) = add(keep, got, True)
        held = [send]
        for bit in reversed(order):
            held = held + [swap(one, bit) for one in held]
        payloads.append(held)
        pairs.append((lax.ppermute(state, "tm", back), forced))
    return (gradient_of(numbers, payloads, rows, cols), starts_of(pairs, rows, cols)[None])


def solution(mesh):
    in_specs = (
        P("tm", "space", None),
        P("space", None),
        P("space", None),
        P("tm"),
        P("tm", "space", None),
    )
    out_specs = (P("space", None), P("tm", "space", None))
    return jax.shard_map(local, mesh=mesh, in_specs=in_specs, out_specs=out_specs, check_vma=False)
```
